32 devices in a mesh: cond: 4 (over y, x), shard: 8 (over z, core).
Axes of the slice: x: 2, y: 2, z: 4, core: 2. Of those that a mesh axis runs over, the one named last changes fastest.
Arguments:
- expression: bfloat16 [2048, 2048], P(('cond', 'shard')), may hold values from -6 to 6
- responses: bfloat16 [2048, 512], P(('cond', 'shard')), may hold values from -200 to 200
- coef_init: float32 [8192, 512], P(('cond', 'shard')), may hold values from -4 to 4
- dual_init: float32 [8192, 512], P(('cond', 'shard')), may hold values from -3 to 3
- penalty: float32 [2048], P('shard'), may hold values from 0.5 to 4
Outputs:
- coefficients: float32 [8192, 512], P(('cond', 'shard'))
- consensus: float32 [8192, 512], P(('cond', 'shard'))
- duals: float32 [8192, 512], P(('cond', 'shard'))
The draws below stay inside these ranges and needn't reach their ends.
All inputs are finite; a program needn't handle non-finite values.
Results may differ from the reference program's by a relative error of at most 0.0045.
Values may be sent and summed in bfloat16 or wider, within the bound.
No kernel may reach another device: no remote copies, remote signals or barrier semaphores. Data moves between devices by JAX's collectives and lax.ppermute only.
A program may use at most 64 MiB of HBM per device.

```python
import math
import jax
import jax.numpy as jnp
from jax import lax

P_SIZE = 2048
TGT = 512
CELLS_DEV = 64
ITERS = 2
N_CONDS = 4
CELLS = 512
N_SHARD = 8


def levels(own_key, shape, cuts, smallest, high):
    def one(axis_at, parts):
        heights = jax.random.uniform(jax.random.fold_in(jax.random.fold_in(own_key, 6), axis_at), (parts,), jnp.float32, smallest / len(cuts), high / len(cuts))
        return jnp.repeat(jnp.exp(heights), shape[axis_at] // parts).reshape((-1,) + (1,) * (len(shape) - axis_at - 1))

    factor_of = one(*cuts[0])
    for cut in cuts[1:]:
        factor_of = factor_of * one(*cut)
    return factor_of


def centred(rng, extent, deviation, bound, shards=(), kind=jnp.bfloat16):
    result = jax.random.normal(rng, extent, jnp.float32) * deviation
    if len(shards) > 0:
        result = levels(rng, extent, shards, -0.22, 0.18) * result
    return jnp.clip(result, min=-bound, max=bound).astype(kind)


def setup_inputs(seed: int = 0) -> dict:
    splits = jax.random.split(jax.random.key(seed), 6)
    return {
        "expression": centred(splits[0], (N_CONDS * CELLS, P_SIZE), 1.0, 6.0, ((0, 32),)),
        "responses": centred(splits[1], (N_CONDS * CELLS, TGT), 32.0, 200.0, ((0, 32),)),
        "coef_init": centred(splits[2], (N_CONDS * P_SIZE, TGT), 0.5, 4.0, ((0, 32),), jnp.float32),
        "dual_init": centred(splits[3], (N_CONDS * P_SIZE, TGT), 0.3, 3.0, ((0, 32),), jnp.float32),
        "penalty": jnp.clip(jnp.exp(math.log(4.0) - 2.0794415 * jax.random.uniform(splits[4], (P_SIZE,), jnp.float32) ** levels(splits[4], (P_SIZE,), ((0, 8),), -0.2, 0.2)), 0.5, 4.0),
    }


rho_weight = 2.0

def reference(expression, responses, coef_init, dual_init, penalty):
    n_cells = CELLS_DEV * N_SHARD
    cell_x = expression.reshape(N_CONDS, n_cells, P_SIZE)
    cell_y = responses.reshape(N_CONDS, n_cells, TGT)

    def gram_one(pair):
        left, right = pair
        gram = jnp.dot(left.T, left, preferred_element_type=jnp.float32) / n_cells
        cross = jnp.dot(left.T, right, preferred_element_type=jnp.float32) / n_cells
        return (gram.astype(jnp.bfloat16), jnp.diagonal(gram), cross)
    gram_copy, diagonal, cross = lax.map(gram_one, (cell_x, cell_y))
    coef = coef_init.reshape(N_CONDS, P_SIZE, TGT)
    dual = dual_init.reshape(N_CONDS, P_SIZE, TGT)
    weights = penalty[None, :, None]
    consensus = coef
    for step in range(ITERS):
        merged = coef + dual
        norms = jnp.sqrt(lax.optimization_barrier(jnp.sum(merged * merged, axis=0)))[None]
        consensus = merged * (1.0 - weights / jnp.maximum(norms, weights))
        dual = merged - consensus
        coef_copy = coef.astype(jnp.bfloat16)
        product = lax.map(lambda pair: jnp.dot(pair[0], pair[1], preferred_element_type=jnp.float32), (gram_copy, coef_copy))
        coef = coef + (cross + rho_weight * (consensus - dual) - product - rho_weight * coef) / (diagonal[:, :, None] + rho_weight)
    return (coef.reshape(N_CONDS * P_SIZE, TGT), consensus.reshape(N_CONDS * P_SIZE, TGT), dual.reshape(N_CONDS * P_SIZE, TGT))
```

```python
import jax
import jax.numpy as jnp
from jax import lax
from jax.sharding import PartitionSpec as P

ITERS = 2


rho_weight = 2.0
bf16 = jnp.bfloat16
f32 = jnp.float32


def bits_of(count):
    return count.bit_length() - 1


def swap(value, axis, mask):
    size = lax.axis_size(axis)
    return lax.ppermute(value, axis, [(i, i ^ mask) for i in range(size)])


def cond_sum(squares):
    bits = range(bits_of(lax.axis_size("cond")))
    half = squares.shape[0] // 2
    parts = [squares[:half], squares[half:]]
    for low, high in zip(bits, reversed(bits)):
        parts = [
            part + swap(part.astype(bf16), "cond", 1 << bit).astype(f32)
            for part, bit in zip(parts, (low, high))
        ]
    return jnp.concatenate(parts)


def shards(expression, responses, coef_init, dual_init, penalty):
    cells, targets = responses.shape
    mine = coef_init.shape[0]
    chips = lax.axis_size("shard") // 2
    n_bits = bits_of(chips)
    n_cells = cells * lax.axis_size("shard")
    me = lax.axis_index("shard")
    chip, core = me // 2, me % 2

    by_chip = expression.reshape(cells, chips, 2, mine)
    own, other = [], []
    for k in range(chips):
        rows = lax.dynamic_index_in_dim(by_chip, chip ^ k, 1, keepdims=False)
        pair = jnp.stack([
            lax.dynamic_index_in_dim(rows, core, 1, keepdims=False),
            lax.dynamic_index_in_dim(rows, 1 - core, 1, keepdims=False),
        ])
        if k > 0:
            pair = swap(pair, "shard", 2 * k)
        own.append(pair[0])
        other.append(pair[1])
    own = jnp.concatenate(own)
    other = jnp.concatenate(other)
    across = swap(other, "shard", 1)

    squares = jnp.sum(jnp.square(own.astype(f32)), 0) + jnp.sum(jnp.square(across.astype(f32)), 0)
    step_size = 1.0 / (squares / n_cells + rho_weight)[:, None]

    coef = coef_init
    dual = dual_init
    weights = penalty[:, None]
    consensus = coef
    for step in range(ITERS):
        merged = coef + dual
        coef_copy = coef.astype(bf16)
        coef_other = swap(coef_copy, "shard", 1)
        total = jnp.dot(own, coef_copy, preferred_element_type=f32) + jnp.dot(
            other, coef_other, preferred_element_type=f32
        )
        total = total.reshape(chips, cells, targets)
        total = jnp.concatenate([total[:1] - responses.astype(f32), total[1:]])
        total = total.reshape([2] * n_bits + [cells, targets])
        for bit in range(n_bits - 1):
            axis = n_bits - 1 - bit
            keep = lax.index_in_dim(total, 0, axis, keepdims=False)
            send = lax.index_in_dim(total, 1, axis, keepdims=False)
            total = keep + swap(send.astype(bf16), "shard", 2 << bit).astype(f32)
        if n_bits > 0:
            last = swap(total[::-1].astype(bf16), "shard", 1 << n_bits)
            total = total + last.astype(f32)
        residual = total.astype(bf16)
        for bit in reversed(range(n_bits - 1)):
            residual = jnp.stack([residual, swap(residual, "shard", 2 << bit)], n_bits - 1 - bit)
        residual = residual.reshape(chips * cells, targets)
        residual_other = swap(residual, "shard", 1)
        contract = (((0,), (0,)), ((), ()))
        product = lax.dot_general(own, residual, contract, preferred_element_type=f32) + lax.dot_general(
            across, residual_other, contract, preferred_element_type=f32
        )

        norms = jnp.sqrt(cond_sum(merged * merged))
        consensus = merged * (1.0 - weights / jnp.maximum(norms, weights))
        dual = merged - consensus
        coef = coef + (rho_weight * (consensus - dual) - product / n_cells - rho_weight * coef) * step_size
    return (coef, consensus, dual)


def solution(mesh):
    in_specs = (
        P(("cond", "shard"), None),
        P(("cond", "shard"), None),
        P(("cond", "shard"), None),
        P(("cond", "shard"), None),
        P("shard"),
    )
    out_specs = (P(("cond", "shard"), None), P(("cond", "shard"), None), P(("cond", "shard"), None))
    return jax.shard_map(shards, mesh=mesh, in_specs=in_specs, out_specs=out_specs, check_vma=False)
```

```python
import jax
import jax.numpy as jnp
from jax import lax
from jax.sharding import PartitionSpec as P

ITERS = 2


rho_weight = 2.0
bf16 = jnp.bfloat16
f32 = jnp.float32


def swap(value, axis, mask, what):
    size = lax.axis_size(axis)
    with jax.named_scope(what):
        return lax.ppermute(value, axis, [(i, i ^ mask) for i in range(size)])


def together(*values):
    return lax.optimization_barrier(values)


def shards(expression, responses, coef_init, dual_init, penalty):
    cells, targets = responses.shape
    mine = coef_init.shape[0]
    chips = lax.axis_size("shard") // 2
    cond_bits = lax.axis_size("cond").bit_length() - 1
    n_cells = cells * lax.axis_size("shard")
    me = lax.axis_index("shard")
    chip, core = me // 2, me % 2
    far_first = list(reversed(range(1, chips)))
    contract = (((0,), (0,)), ((), ()))

    def dot(x, c):
        return jnp.dot(x, c, preferred_element_type=f32)

    def columns(k, side):
        start = ((chip ^ k) * 2 + (core ^ side)) * mine
        return lax.dynamic_slice_in_dim(expression, start, mine, 1)

    coef_copy = coef_init.astype(bf16)
    coef_other = swap(coef_copy, "shard", 1, "coef_core")
    pairs = [jnp.stack([columns(k, 0), columns(k, 1)]) for k in range(chips)]
    for k in far_first:
        pairs[k] = swap(pairs[k], "shard", 2 * k, f"cells{k}")
    weights = jnp.broadcast_to(penalty[:, None], coef_init.shape)
    response_rows = responses.astype(f32)
    pairs, weights, response_rows = together(pairs, weights, response_rows)
    own = jnp.concatenate([p[0] for p in pairs])
    other = jnp.concatenate([p[1] for p in pairs])

    coef = coef_init
    dual = dual_init
    for step in range(ITERS):
        merged = coef + dual
        squares = merged * merged
        if cond_bits > 0:
            squares = squares + swap(squares.astype(bf16), "cond", 1, "squares0").astype(f32)
        if step > 0:
            coef_copy = coef.astype(bf16)
            coef_other = swap(coef_copy, "shard", 1, "coef_core")
        fitted = (dot(own, coef_copy) + dot(other, coef_other)).reshape(chips, cells, targets)
        total = fitted[0] - response_rows
        leaving = fitted.astype(bf16)
        leaving, total, held, squares = together(leaving, total, other, squares) if step == 0 else (*together(leaving, total), other, squares)
        arrived = [swap(leaving[k], "shard", 2 * k, f"fit{k}") for k in far_first]
        for bit in range(1, cond_bits):
            squares = squares + swap(squares.astype(bf16), "cond", 1 << bit, f"squares{bit}").astype(f32)
        for part in arrived:
            total = total + part.astype(f32)
        residual = [total.astype(bf16)] * chips
        for k in far_first:
            residual[k] = swap(residual[0], "shard", 2 * k, f"residual{k}")
        if step == 0:
            across = swap(held, "shard", 1, "cells_core")
            diagonal = jnp.sum(jnp.square(own.astype(f32)), 0) + jnp.sum(jnp.square(across.astype(f32)), 0)
            step_size = 1.0 / (diagonal / n_cells + rho_weight)[:, None]
            residual, squares, step_size, across = together(residual, squares, step_size, across)
        else:
            residual, squares = together(residual, squares)
        residual = jnp.concatenate(residual)
        residual_other = swap(residual, "shard", 1, "residual_core")
        product = lax.dot_general(own, residual, contract, preferred_element_type=f32) + lax.dot_general(
            across, residual_other, contract, preferred_element_type=f32
        )

        norms = jnp.sqrt(squares)
        consensus = merged * (1.0 - weights / jnp.maximum(norms, weights))
        dual = merged - consensus
        coef = coef + (rho_weight * (consensus - dual) - product / n_cells - rho_weight * coef) * step_size
    return (coef, consensus, dual)


def solution(mesh):
    in_specs = (
        P(("cond", "shard"), None),
        P(("cond", "shard"), None),
        P(("cond", "shard"), None),
        P(("cond", "shard"), None),
        P("shard"),
    )
    out_specs = (P(("cond", "shard"), None), P(("cond", "shard"), None), P(("cond", "shard"), None))
    return jax.shard_map(shards, mesh=mesh, in_specs=in_specs, out_specs=out_specs, check_vma=False)
```

```python
import jax
import jax.numpy as jnp
from jax import lax
from jax.sharding import PartitionSpec as P

ITERS = 2


rho_weight = 2.0
bf16 = jnp.bfloat16
f32 = jnp.float32


def bits_of(size):
    return size.bit_length() - 1


def mirrored(mask, bits):
    return sum(((mask >> b) & 1) << (bits - 1 - b) for b in range(bits))


def core_swap(value, what):
    with jax.named_scope(what):
        return lax.ppermute(value, "shard", [(i, i ^ 1) for i in range(lax.axis_size("shard"))])


def chip_swap(value, mask, what):
    with jax.named_scope(what):
        return lax.ppermute(value, "shard", [(i, i ^ (2 * mask)) for i in range(lax.axis_size("shard"))])


def cond_swap(value, mask, what):
    conds, size = lax.axis_size("cond"), lax.axis_size("shard")
    masks = (mask, mirrored(mask, bits_of(conds)))
    pairs = [(c * size + i, (c ^ masks[i % 2]) * size + i) for c in range(conds) for i in range(size)]
    with jax.named_scope(what):
        return lax.ppermute(value, ("cond", "shard"), pairs)


def together(*values):
    return lax.optimization_barrier(values)


def shards(expression, responses, coef_init, dual_init, penalty):
    cells, targets = responses.shape
    mine = coef_init.shape[0]
    chips = lax.axis_size("shard") // 2
    cond_bits = bits_of(lax.axis_size("cond"))
    n_cells = cells * lax.axis_size("shard")
    me = lax.axis_index("shard")
    chip, core = me // 2, me % 2
    far_first = list(reversed(range(1, chips)))
    contract = (((0,), (0,)), ((), ()))

    def dot(x, c):
        return jnp.dot(x, c, preferred_element_type=f32)

    def columns(k, side):
        start = ((chip ^ k) * 2 + (core ^ side)) * mine
        return lax.dynamic_slice_in_dim(expression, start, mine, 1)

    coef_copy = coef_init.astype(bf16)
    coef_other = core_swap(coef_copy, "coef_core")
    pairs = [jnp.stack([columns(k, 0), columns(k, 1)]) for k in range(chips)]
    for k in far_first:
        pairs[k] = chip_swap(pairs[k], k, f"cells{k}")
    weights = jnp.broadcast_to(penalty[:, None], coef_init.shape)
    response_rows = responses.astype(f32)
    order = [0] + far_first
    *ordered, weights, response_rows = together(*[pairs[k] for k in order], weights, response_rows)
    for k, pair in zip(order, ordered):
        pairs[k] = pair
    own = jnp.concatenate([pairs[k][0] for k in order])
    other = jnp.concatenate([pairs[k][1] for k in order])

    coef = coef_init
    dual = dual_init
    for step in range(ITERS):
        merged = coef + dual
        squares = merged * merged
        if cond_bits > 0:
            squares = squares + cond_swap(squares.astype(bf16), 1, "squares0").astype(f32)
        if step > 0:
            coef_copy = coef.astype(bf16)
            coef_other = core_swap(coef_copy, "coef_core")
        fitted = (dot(own, coef_copy) + dot(other, coef_other)).reshape(chips, cells, targets)
        total = fitted[0] - response_rows
        leaving = fitted.astype(bf16)
        held = other
        if step == 0:
            leaving, total, held, squares = together(leaving, total, held, squares)
        arrived = [chip_swap(leaving[order.index(k)], k, f"fit{k}") for k in far_first]
        for bit in range(1, cond_bits):
            squares = squares + cond_swap(squares.astype(bf16), 1 << bit, f"squares{bit}").astype(f32)
        for part in arrived:
            total = total + part.astype(f32)
        residual = [total.astype(bf16)] * chips
        for k in far_first:
            residual[k] = chip_swap(residual[0], k, f"residual{k}")
        if step == 0:
            across = core_swap(held, "cells_core")
            diagonal = jnp.sum(jnp.square(own.astype(f32)), 0) + jnp.sum(jnp.square(across.astype(f32)), 0)
            step_size = 1.0 / (diagonal / n_cells + rho_weight)[:, None]
            residual, squares, step_size, across = together(residual, squares, step_size, across)
        else:
            residual, squares = together(residual, squares)
        residual = jnp.concatenate([residual[k] for k in order])
        residual_other = core_swap(residual, "residual_core")
        product = lax.dot_general(own, residual, contract, preferred_element_type=f32) + lax.dot_general(
            across, residual_other, contract, preferred_element_type=f32
        )

        norms = jnp.sqrt(squares)
        consensus = merged * (1.0 - weights / jnp.maximum(norms, weights))
        dual = merged - consensus
        coef = coef + (rho_weight * (consensus - dual) - product / n_cells - rho_weight * coef) * step_size
    return (coef, consensus, dual)


def solution(mesh):
    in_specs = (
        P(("cond", "shard"), None),
        P(("cond", "shard"), None),
        P(("cond", "shard"), None),
        P(("cond", "shard"), None),
        P("shard"),
    )
    out_specs = (P(("cond", "shard"), None), P(("cond", "shard"), None), P(("cond", "shard"), None))
    return jax.shard_map(shards, mesh=mesh, in_specs=in_specs, out_specs=out_specs, check_vma=False)
```

```python
import jax
import jax.numpy as jnp
from jax import lax
from jax.sharding import PartitionSpec as P

ITERS = 2


rho_weight = 2.0
bf16 = jnp.bfloat16
f32 = jnp.float32


def bits_of(size):
    return size.bit_length() - 1


def mirrored(mask, bits):
    return sum(((mask >> b) & 1) << (bits - 1 - b) for b in range(bits))


def core_swap(value, what):
    with jax.named_scope(what):
        return lax.ppermute(value, "shard", [(i, i ^ 1) for i in range(lax.axis_size("shard"))])


def chip_swap(value, mask, what):
    with jax.named_scope(what):
        return lax.ppermute(value, "shard", [(i, i ^ (2 * mask)) for i in range(lax.axis_size("shard"))])


def cond_swap(value, mask, what):
    conds, size = lax.axis_size("cond"), lax.axis_size("shard")
    masks = (mask, mirrored(mask, bits_of(conds)))
    pairs = [(c * size + i, (c ^ masks[i % 2]) * size + i) for c in range(conds) for i in range(size)]
    with jax.named_scope(what):
        return lax.ppermute(value, ("cond", "shard"), pairs)


def together(*values):
    return lax.optimization_barrier(values)


def shards(expression, responses, coef_init, dual_init, penalty):
    cells, targets = responses.shape
    mine = coef_init.shape[0]
    chips = lax.axis_size("shard") // 2
    cond_bits = bits_of(lax.axis_size("cond"))
    n_cells = cells * lax.axis_size("shard")
    me = lax.axis_index("shard")
    chip, core = me // 2, me % 2
    far_first = list(reversed(range(1, chips)))
    contract = (((0,), (0,)), ((), ()))

    def dot(x, c):
        return jnp.dot(x, c, preferred_element_type=f32)

    def columns(k, side):
        start = ((chip ^ k) * 2 + (core ^ side)) * mine
        return lax.dynamic_slice_in_dim(expression, start, mine, 1)

    coef_copy = coef_init.astype(bf16)
    coef_other = core_swap(coef_copy, "coef_core")
    pairs = [jnp.stack([columns(k, 0), columns(k, 1)]) for k in range(chips)]
    for k in far_first:
        pairs[k] = chip_swap(pairs[k], k, f"cells{k}")
    weights = jnp.broadcast_to(penalty[:, None], coef_init.shape)
    response_rows = responses.astype(f32)

    def fit(k):
        return dot(pairs[k][0], coef_copy) + dot(pairs[k][1], coef_other)

    total = fit(0)
    leaving = {}
    before = ()
    for k in far_first:
        if before:
            pairs[k], *_ = together(pairs[k], *before)
        leaving[k] = fit(k).astype(bf16)
        before = (leaving[k],)
    order = [0] + far_first
    own = jnp.concatenate([pairs[k][0] for k in order])
    other = jnp.concatenate([pairs[k][1] for k in order])

    coef = coef_init
    dual = dual_init
    for step in range(ITERS):
        merged = coef + dual
        squares = merged * merged
        if cond_bits > 0:
            squares = squares + cond_swap(squares.astype(bf16), 1, "squares0").astype(f32)
        if step > 0:
            coef_copy = coef.astype(bf16)
            coef_other = core_swap(coef_copy, "coef_core")
            fitted = (dot(own, coef_copy) + dot(other, coef_other)).reshape(chips, cells, targets)
            total = fitted[0]
            leaving = {k: fitted[order.index(k)].astype(bf16) for k in far_first}
        else:
            held, squares, weights, response_rows, *_ = together(other, squares, weights, response_rows, *before)
        arrived = [chip_swap(leaving[k], k, f"fit{k}") for k in far_first]
        for bit in range(1, cond_bits):
            squares = squares + cond_swap(squares.astype(bf16), 1 << bit, f"squares{bit}").astype(f32)
        total = total - response_rows
        for part in arrived:
            total = total + part.astype(f32)
        residual = [total.astype(bf16)] * chips
        for k in far_first:
            residual[k] = chip_swap(residual[0], k, f"residual{k}")
        if step == 0:
            across = core_swap(held, "cells_core")
            diagonal = jnp.sum(jnp.square(own.astype(f32)), 0) + jnp.sum(jnp.square(across.astype(f32)), 0)
            step_size = 1.0 / (diagonal / n_cells + rho_weight)[:, None]
            residual, squares, step_size, across = together(residual, squares, step_size, across)
        else:
            residual, squares = together(residual, squares)
        residual = jnp.concatenate([residual[k] for k in order])
        residual_other = core_swap(residual, "residual_core")
        product = lax.dot_general(own, residual, contract, preferred_element_type=f32) + lax.dot_general(
            across, residual_other, contract, preferred_element_type=f32
        )

        norms = jnp.sqrt(squares)
        consensus = merged * (1.0 - weights / jnp.maximum(norms, weights))
        dual = merged - consensus
        coef = coef + (rho_weight * (consensus - dual) - product / n_cells - rho_weight * coef) * step_size
    return (coef, consensus, dual)


def solution(mesh):
    in_specs = (
        P(("cond", "shard"), None),
        P(("cond", "shard"), None),
        P(("cond", "shard"), None),
        P(("cond", "shard"), None),
        P("shard"),
    )
    out_specs = (P(("cond", "shard"), None), P(("cond", "shard"), None), P(("cond", "shard"), None))
    return jax.shard_map(shards, mesh=mesh, in_specs=in_specs, out_specs=out_specs, check_vma=False)
```

```python
import jax
import jax.numpy as jnp
from jax import lax
from jax.sharding import PartitionSpec as P

ITERS = 2


rho_weight = 2.0
bf16 = jnp.bfloat16
f32 = jnp.float32


def bits_of(size):
    return size.bit_length() - 1


def mirrored(mask, bits):
    return sum(((mask >> b) & 1) << (bits - 1 - b) for b in range(bits))


def core_swap(value, what):
    with jax.named_scope(what):
        return lax.ppermute(value, "shard", [(i, i ^ 1) for i in range(lax.axis_size("shard"))])


def chip_swap(value, mask, what):
    with jax.named_scope(what):
        return lax.ppermute(value, "shard", [(i, i ^ (2 * mask)) for i in range(lax.axis_size("shard"))])


def cond_swap(value, mask, what):
    conds, size = lax.axis_size("cond"), lax.axis_size("shard")
    masks = (mask, mirrored(mask, bits_of(conds)))
    pairs = [(c * size + i, (c ^ masks[i % 2]) * size + i) for c in range(conds) for i in range(size)]
    with jax.named_scope(what):
        return lax.ppermute(value, ("cond", "shard"), pairs)


def together(*values):
    return lax.optimization_barrier(values)


def shards(expression, responses, coef_init, dual_init, penalty):
    cells, targets = responses.shape
    mine = coef_init.shape[0]
    chips = lax.axis_size("shard") // 2
    cond_bits = bits_of(lax.axis_size("cond"))
    n_cells = cells * lax.axis_size("shard")
    me = lax.axis_index("shard")
    chip, core = me // 2, me % 2
    far_first = list(reversed(range(1, chips)))
    order = [0] + far_first
    evens_first = sorted(range(chips), key=lambda k: (k > 0, k % 2, k))
    contract = (((0,), (0,)), ((), ()))

    def dot(x, c):
        return jnp.dot(x, c, preferred_element_type=f32)

    def columns(k, side):
        start = ((chip ^ k) * 2 + (core ^ side)) * mine
        return lax.dynamic_slice_in_dim(expression, start, mine, 1)

    (coef_copy,) = together(coef_init.astype(bf16))
    coef_other = core_swap(coef_copy, "coef_core")
    pairs = [jnp.stack([columns(k, 0), columns(k, 1)]) for k in range(chips)]
    for k in far_first:
        pairs[k] = chip_swap(pairs[k], k, f"cells{k}")
    weights = jnp.broadcast_to(penalty[:, None], coef_init.shape)
    response_rows = responses.astype(f32)

    def fit(k):
        return dot(pairs[k][0], coef_copy) + dot(pairs[k][1], coef_other)

    total = fit(0)
    leaving = {}
    before = ()
    for k in far_first:
        if before:
            pairs[k], *_ = together(pairs[k], *before)
        leaving[k] = fit(k).astype(bf16)
        before = (leaving[k],)
    own = jnp.concatenate([pairs[k][0] for k in order])
    other = jnp.concatenate([pairs[k][1] for k in order])

    coef = coef_init
    dual = dual_init
    for step in range(ITERS):
        merged = coef + dual
        squares = merged * merged
        if cond_bits > 0:
            squares = squares + cond_swap(squares.astype(bf16), 1, "squares0").astype(f32)
        if step == 0:
            held, squares, weights, response_rows, *_ = together(other, squares, weights, response_rows, *before)
        else:
            coef_copy = coef.astype(bf16)
            coef_other = core_swap(coef_copy, "coef_core")
            fitted = (dot(own, coef_copy) + dot(other, coef_other)).reshape(chips, cells, targets)
            total = fitted[0]
            leaving = {k: fitted[order.index(k)].astype(bf16) for k in far_first}
        arrived = [chip_swap(leaving[k], k, f"fit{k}") for k in far_first]
        for bit in range(1, cond_bits):
            squares = squares + cond_swap(squares.astype(bf16), 1 << bit, f"squares{bit}").astype(f32)
        total = total - response_rows
        for part in arrived:
            total = total + part.astype(f32)
        residual = [total.astype(bf16)] * chips
        for k in far_first:
            residual[k] = chip_swap(residual[0], k, f"residual{k}")
        if step == 0:
            across = core_swap(held, "cells_core")
            diagonal = jnp.sum(jnp.square(own.astype(f32)), 0) + jnp.sum(jnp.square(across.astype(f32)), 0)
            step_size = 1.0 / (diagonal / n_cells + rho_weight)[:, None]
        squares, step_size, across, *ready = together(squares, step_size, across, *[residual[k] for k in evens_first])
        residual = dict(zip(evens_first, ready))
        residual = jnp.concatenate([residual[k] for k in order])
        residual_other = core_swap(residual, "residual_core")
        product = lax.dot_general(own, residual, contract, preferred_element_type=f32) + lax.dot_general(
            across, residual_other, contract, preferred_element_type=f32
        )

        norms = jnp.sqrt(squares)
        consensus = merged * (1.0 - weights / jnp.maximum(norms, weights))
        dual = merged - consensus
        coef = coef + (rho_weight * (consensus - dual) - product / n_cells - rho_weight * coef) * step_size
    return (coef, consensus, dual)


def solution(mesh):
    in_specs = (
        P(("cond", "shard"), None),
        P(("cond", "shard"), None),
        P(("cond", "shard"), None),
        P(("cond", "shard"), None),
        P("shard"),
    )
    out_specs = (P(("cond", "shard"), None), P(("cond", "shard"), None), P(("cond", "shard"), None))
    return jax.shard_map(shards, mesh=mesh, in_specs=in_specs, out_specs=out_specs, check_vma=False)
```

```python
import jax
import jax.numpy as jnp
from jax import lax
from jax.sharding import PartitionSpec as P

ITERS = 2


rho_weight = 2.0
bf16 = jnp.bfloat16
f32 = jnp.float32


def bits_of(size):
    return size.bit_length() - 1


def mirrored(mask, bits):
    return sum(((mask >> b) & 1) << (bits - 1 - b) for b in range(bits))


def core_swap(value, what):
    with jax.named_scope(what):
        return lax.ppermute(value, "shard", [(i, i ^ 1) for i in range(lax.axis_size("shard"))])


def chip_swap(value, mask, what):
    with jax.named_scope(what):
        return lax.ppermute(value, "shard", [(i, i ^ (2 * mask)) for i in range(lax.axis_size("shard"))])


def cond_swap(value, mask, what):
    conds, size = lax.axis_size("cond"), lax.axis_size("shard")
    masks = (mask, mirrored(mask, bits_of(conds)))
    pairs = [(c * size + i, (c ^ masks[i % 2]) * size + i) for c in range(conds) for i in range(size)]
    with jax.named_scope(what):
        return lax.ppermute(value, ("cond", "shard"), pairs)


def together(*values):
    return lax.optimization_barrier(values)


def shards(expression, responses, coef_init, dual_init, penalty):
    cells, targets = responses.shape
    mine = coef_init.shape[0]
    chips = lax.axis_size("shard") // 2
    cond_bits = bits_of(lax.axis_size("cond"))
    n_cells = cells * lax.axis_size("shard")
    me = lax.axis_index("shard")
    chip, core = me // 2, me % 2
    far_first = list(reversed(range(1, chips)))
    order = [0] + far_first
    evens_first = sorted(range(chips), key=lambda k: (k > 0, k % 2, k))
    contract = (((0,), (0,)), ((), ()))

    def dot(x, c):
        return jnp.dot(x, c, preferred_element_type=f32)

    def columns(k, side):
        start = ((chip ^ k) * 2 + (core ^ side)) * mine
        return lax.dynamic_slice_in_dim(expression, start, mine, 1)

    (coef_copy,) = together(coef_init.astype(bf16))
    coef_other = core_swap(coef_copy, "coef_core")
    pairs = [jnp.stack([columns(k, 0), columns(k, 1)]) for k in range(chips)]
    for k in far_first:
        pairs[k] = chip_swap(pairs[k], k, f"cells{k}")
    weights = jnp.broadcast_to(penalty[:, None], coef_init.shape)
    response_rows = responses.astype(f32)

    def fit(k):
        return dot(pairs[k][0], coef_copy) + dot(pairs[k][1], coef_other)

    total = fit(0)
    leaving = {}
    before = ()
    for k in far_first:
        if before:
            pairs[k], *_ = together(pairs[k], *before)
        leaving[k] = fit(k).astype(bf16)
        before = (leaving[k],)
    own = jnp.concatenate([pairs[k][0] for k in order])
    other = jnp.concatenate([pairs[k][1] for k in order])

    coef = coef_init
    dual = dual_init
    for step in range(ITERS):
        merged = coef + dual
        squares = merged * merged
        if cond_bits > 0:
            squares = squares + cond_swap(squares.astype(bf16), 1, "squares0").astype(f32)
        if step == 0:
            held, squares, weights, response_rows, *_ = together(other, squares, weights, response_rows, *before)
        else:
            coef_copy = coef.astype(bf16)
            coef_other = core_swap(coef_copy, "coef_core")
            fitted = (dot(own, coef_copy) + dot(other, coef_other)).reshape(chips, cells, targets)
            total = fitted[0]
            leaving = {k: fitted[order.index(k)].astype(bf16) for k in far_first}
        arrived = [chip_swap(leaving[k], k, f"fit{k}") for k in far_first]
        for bit in range(1, cond_bits):
            squares = squares + cond_swap(squares.astype(bf16), 1 << bit, f"squares{bit}").astype(f32)
        total = total - response_rows
        for part in arrived:
            total = total + part.astype(f32)
        residual = [total.astype(bf16)] * chips
        for k in far_first:
            residual[k] = chip_swap(residual[0], k, f"residual{k}")
        if step == 0:
            across = core_swap(held, "cells_core")
            diagonal = jnp.sum(jnp.square(own.astype(f32)), 0) + jnp.sum(jnp.square(across.astype(f32)), 0)
            step_size = 1.0 / (diagonal / n_cells + rho_weight)[:, None]
        squares, step_size, across, *ready = together(squares, step_size, across, *[residual[k] for k in evens_first])
        residual = dict(zip(evens_first, ready))
        residual = jnp.concatenate([residual[k] for k in order])
        residual_other = core_swap(residual, "residual_core")
        norms = jnp.sqrt(squares)
        consensus = merged * (1.0 - weights / jnp.maximum(norms, weights))
        dual = merged - consensus
        scale = step_size / n_cells
        coef = coef + (rho_weight * (consensus - dual) - rho_weight * coef) * step_size
        coef = coef - lax.dot_general(own, residual, contract, preferred_element_type=f32) * scale
        if step < ITERS - 1:
            residual_other, coef, dual = together(residual_other, coef, dual)
        coef = coef - lax.dot_general(across, residual_other, contract, preferred_element_type=f32) * scale
    return (coef, consensus, dual)


def solution(mesh):
    in_specs = (
        P(("cond", "shard"), None),
        P(("cond", "shard"), None),
        P(("cond", "shard"), None),
        P(("cond", "shard"), None),
        P("shard"),
    )
    out_specs = (P(("cond", "shard"), None), P(("cond", "shard"), None), P(("cond", "shard"), None))
    return jax.shard_map(shards, mesh=mesh, in_specs=in_specs, out_specs=out_specs, check_vma=False)
```

```python
import jax
import jax.numpy as jnp
from jax import lax
from jax.sharding import PartitionSpec as P

ITERS = 2


rho_weight = 2.0
bf16 = jnp.bfloat16
f32 = jnp.float32


def bits_of(size):
    return size.bit_length() - 1


def mirrored(mask, bits):
    return sum(((mask >> b) & 1) << (bits - 1 - b) for b in range(bits))


def core_swap(value, what):
    with jax.named_scope(what):
        return lax.ppermute(value, "shard", [(i, i ^ 1) for i in range(lax.axis_size("shard"))])


def chip_swap(value, mask, what):
    with jax.named_scope(what):
        return lax.ppermute(value, "shard", [(i, i ^ (2 * mask)) for i in range(lax.axis_size("shard"))])


def cond_swap(value, mask, what):
    conds, size = lax.axis_size("cond"), lax.axis_size("shard")
    masks = (mirrored(mask, bits_of(conds)), mask)
    pairs = [(c * size + i, (c ^ masks[i % 2]) * size + i) for c in range(conds) for i in range(size)]
    with jax.named_scope(what):
        return lax.ppermute(value, ("cond", "shard"), pairs)


def together(*values):
    return lax.optimization_barrier(values)


def shards(expression, responses, coef_init, dual_init, penalty):
    cells, targets = responses.shape
    mine = coef_init.shape[0]
    chips = lax.axis_size("shard") // 2
    cond_bits = bits_of(lax.axis_size("cond"))
    n_cells = cells * lax.axis_size("shard")
    me = lax.axis_index("shard")
    chip, core = me // 2, me % 2
    far_first = list(reversed(range(1, chips)))
    order = [0] + far_first
    evens_first = sorted(range(chips), key=lambda k: (k > 0, k % 2, k))
    contract = (((0,), (0,)), ((), ()))

    def dot(x, c):
        return jnp.dot(x, c, preferred_element_type=f32)

    def columns(k, side):
        start = ((chip ^ k) * 2 + (core ^ side)) * mine
        return lax.dynamic_slice_in_dim(expression, start, mine, 1)

    (coef_copy,) = together(coef_init.astype(bf16))
    coef_other = core_swap(coef_copy, "coef_core")
    pairs = [jnp.stack([columns(k, 0), columns(k, 1)]) for k in range(chips)]
    for k in far_first:
        pairs[k] = chip_swap(pairs[k], k, f"cells{k}")
    weights = jnp.broadcast_to(penalty[:, None], coef_init.shape)
    response_rows = responses.astype(f32)

    def fit(k):
        return dot(pairs[k][0], coef_copy) + dot(pairs[k][1], coef_other)

    total = fit(0)
    leaving = {}
    before = ()
    for k in far_first:
        if before:
            pairs[k], *_ = together(pairs[k], *before)
        leaving[k] = fit(k).astype(bf16)
        before = (leaving[k],)
    own = jnp.concatenate([pairs[k][0] for k in order])
    other = jnp.concatenate([pairs[k][1] for k in order])

    coef = coef_init
    dual = dual_init
    for step in range(ITERS):
        merged = coef + dual
        squares = merged * merged
        if cond_bits > 0:
            squares = squares + cond_swap(squares.astype(bf16), 1, "squares0").astype(f32)
        if step == 0:
            held, squares, weights, response_rows, *_ = together(other, squares, weights, response_rows, *before)
        else:
            coef_copy = coef.astype(bf16)
            coef_other = core_swap(coef_copy, "coef_core")
            fitted = (dot(own, coef_copy) + dot(other, coef_other)).reshape(chips, cells, targets)
            total = fitted[0]
            leaving = {k: fitted[order.index(k)].astype(bf16) for k in far_first}
        arrived = [chip_swap(leaving[k], k, f"fit{k}") for k in far_first]
        for bit in range(1, cond_bits):
            squares = squares + cond_swap(squares.astype(bf16), 1 << bit, f"squares{bit}").astype(f32)
        total = total - response_rows
        for part in arrived:
            total = total + part.astype(f32)
        residual = [total.astype(bf16)] * chips
        for k in far_first:
            residual[k] = chip_swap(residual[0], k, f"residual{k}")
        if step == 0:
            across = core_swap(held, "cells_core")
            diagonal = jnp.sum(jnp.square(own.astype(f32)), 0) + jnp.sum(jnp.square(across.astype(f32)), 0)
            step_size = 1.0 / (diagonal / n_cells + rho_weight)[:, None]
        squares, step_size, across, *ready = together(squares, step_size, across, *[residual[k] for k in evens_first])
        residual = dict(zip(evens_first, ready))
        residual = jnp.concatenate([residual[k] for k in order])
        residual_other = core_swap(residual, "residual_core")
        norms = jnp.sqrt(squares)
        consensus = merged * (1.0 - weights / jnp.maximum(norms, weights))
        dual = merged - consensus
        scale = step_size / n_cells
        coef = coef + (rho_weight * (consensus - dual) - rho_weight * coef) * step_size
        coef = coef - lax.dot_general(own, residual, contract, preferred_element_type=f32) * scale
        if step < ITERS - 1:
            residual_other, coef, dual = together(residual_other, coef, dual)
        coef = coef - lax.dot_general(across, residual_other, contract, preferred_element_type=f32) * scale
    return (coef, consensus, dual)


def solution(mesh):
    in_specs = (
        P(("cond", "shard"), None),
        P(("cond", "shard"), None),
        P(("cond", "shard"), None),
        P(("cond", "shard"), None),
        P("shard"),
    )
    out_specs = (P(("cond", "shard"), None), P(("cond", "shard"), None), P(("cond", "shard"), None))
    return jax.shard_map(shards, mesh=mesh, in_specs=in_specs, out_specs=out_specs, check_vma=False)
```

```python
import jax
import jax.numpy as jnp
from jax import lax
from jax.sharding import PartitionSpec as P

ITERS = 2


rho_weight = 2.0
bf16 = jnp.bfloat16
f32 = jnp.float32


def bits_of(size):
    return size.bit_length() - 1


def mirrored(mask, bits):
    return sum(((mask >> b) & 1) << (bits - 1 - b) for b in range(bits))


def core_swap(value, what):
    with jax.named_scope(what):
        return lax.ppermute(value, "shard", [(i, i ^ 1) for i in range(lax.axis_size("shard"))])


def chip_swap(value, mask, what):
    with jax.named_scope(what):
        return lax.ppermute(value, "shard", [(i, i ^ (2 * mask)) for i in range(lax.axis_size("shard"))])


def cond_swap(value, mask, what):
    conds, size = lax.axis_size("cond"), lax.axis_size("shard")
    masks = (mask, mirrored(mask, bits_of(conds)))
    pairs = [(c * size + i, (c ^ masks[i % 2]) * size + i) for c in range(conds) for i in range(size)]
    with jax.named_scope(what):
        return lax.ppermute(value, ("cond", "shard"), pairs)


def together(*values):
    return lax.optimization_barrier(values)


def shards(expression, responses, coef_init, dual_init, penalty):
    cells, targets = responses.shape
    mine = coef_init.shape[0]
    chips = lax.axis_size("shard") // 2
    cond_bits = bits_of(lax.axis_size("cond"))
    n_cells = cells * lax.axis_size("shard")
    me = lax.axis_index("shard")
    chip, core = me // 2, me % 2
    far_first = list(reversed(range(1, chips)))
    order = [0] + far_first
    evens_first = sorted(range(chips), key=lambda k: (k > 0, k % 2, k))
    contract = (((0,), (0,)), ((), ()))

    def dot(x, c):
        return jnp.dot(x, c, preferred_element_type=f32)

    def columns(k, side):
        start = ((chip ^ k) * 2 + (core ^ side)) * mine
        return lax.dynamic_slice_in_dim(expression, start, mine, 1)

    (coef_copy,) = together(coef_init.astype(bf16))
    coef_other = core_swap(coef_copy, "coef_core")
    pairs = [jnp.stack([columns(k, 0), columns(k, 1)]) for k in range(chips)]
    for k in far_first:
        pairs[k] = chip_swap(pairs[k], k, f"cells{k}")
    weights = jnp.broadcast_to(penalty[:, None], coef_init.shape)
    response_rows = responses.astype(f32)

    def fit(k):
        return dot(pairs[k][0], coef_copy) + dot(pairs[k][1], coef_other)

    total = fit(0)
    leaving = {}
    before = ()
    for k in far_first:
        if before:
            pairs[k], *_ = together(pairs[k], *before)
        leaving[k] = fit(k).astype(bf16)
        before = (leaving[k],)
    own = jnp.concatenate([pairs[k][0] for k in order])
    other = jnp.concatenate([pairs[k][1] for k in order])

    coef = coef_init
    dual = dual_init
    for step in range(ITERS):
        merged = coef + dual
        squares = merged * merged
        if cond_bits > 0:
            squares = squares + cond_swap(squares.astype(bf16), 1, "squares0").astype(f32)
        if step == 0:
            held, squares, response_rows, *_ = together(other, squares, response_rows, *before)
        else:
            coef_copy = coef.astype(bf16)
            coef_other = core_swap(coef_copy, "coef_core")
            fitted = (dot(own, coef_copy) + dot(other, coef_other)).reshape(chips, cells, targets)
            total = fitted[0]
            leaving = {k: fitted[order.index(k)].astype(bf16) for k in far_first}
        arrived = [chip_swap(leaving[k], k, f"fit{k}") for k in far_first]
        for bit in range(1, cond_bits):
            squares = squares + cond_swap(squares.astype(bf16), 1 << bit, f"squares{bit}").astype(f32)
        total = total - response_rows
        for part in arrived:
            total = total + part.astype(f32)
        residual = [total.astype(bf16)] * chips
        for k in far_first:
            residual[k] = chip_swap(residual[0], k, f"residual{k}")
        if step == 0:
            across = core_swap(held, "cells_core")
            diagonal = jnp.sum(jnp.square(own.astype(f32)), 0) + jnp.sum(jnp.square(across.astype(f32)), 0)
            step_size = 1.0 / (diagonal / n_cells + rho_weight)[:, None]
        squares, step_size, across, weights, *ready = together(squares, step_size, across, weights, *[residual[k] for k in evens_first])
        residual = dict(zip(evens_first, ready))
        residual = jnp.concatenate([residual[k] for k in order])
        residual_other = core_swap(residual, "residual_core")
        norms = jnp.sqrt(squares)
        consensus = merged * (1.0 - weights / jnp.maximum(norms, weights))
        dual = merged - consensus
        scale = step_size / n_cells
        coef = coef + (rho_weight * (consensus - dual) - rho_weight * coef) * step_size
        coef = coef - lax.dot_general(own, residual, contract, preferred_element_type=f32) * scale
        if step < ITERS - 1:
            residual_other, coef, dual = together(residual_other, coef, dual)
        coef = coef - lax.dot_general(across, residual_other, contract, preferred_element_type=f32) * scale
    return (coef, consensus, dual)


def solution(mesh):
    in_specs = (
        P(("cond", "shard"), None),
        P(("cond", "shard"), None),
        P(("cond", "shard"), None),
        P(("cond", "shard"), None),
        P("shard"),
    )
    out_specs = (P(("cond", "shard"), None), P(("cond", "shard"), None), P(("cond", "shard"), None))
    return jax.shard_map(shards, mesh=mesh, in_specs=in_specs, out_specs=out_specs, check_vma=False)
```

```python
import jax
import jax.numpy as jnp
from jax import lax
from jax.sharding import PartitionSpec as P

ITERS = 2


rho_weight = 2.0
bf16 = jnp.bfloat16
f32 = jnp.float32


def bits_of(size):
    return size.bit_length() - 1


def mirrored(mask, bits):
    return sum(((mask >> b) & 1) << (bits - 1 - b) for b in range(bits))


def core_swap(value, what):
    with jax.named_scope(what):
        return lax.ppermute(value, "shard", [(i, i ^ 1) for i in range(lax.axis_size("shard"))])


def chip_swap(value, mask, what):
    with jax.named_scope(what):
        return lax.ppermute(value, "shard", [(i, i ^ (2 * mask)) for i in range(lax.axis_size("shard"))])


def cond_swap(value, mask, what):
    conds, size = lax.axis_size("cond"), lax.axis_size("shard")
    masks = (mask, mirrored(mask, bits_of(conds)))
    pairs = [(c * size + i, (c ^ masks[i % 2]) * size + i) for c in range(conds) for i in range(size)]
    with jax.named_scope(what):
        return lax.ppermute(value, ("cond", "shard"), pairs)


def together(*values):
    return lax.optimization_barrier(values)


def shards(expression, responses, coef_init, dual_init, penalty):
    cells, targets = responses.shape
    mine = coef_init.shape[0]
    chips = lax.axis_size("shard") // 2
    cond_bits = bits_of(lax.axis_size("cond"))
    n_cells = cells * lax.axis_size("shard")
    me = lax.axis_index("shard")
    chip, core = me // 2, me % 2
    far_first = list(reversed(range(1, chips)))
    order = [0] + far_first
    evens_first = sorted(range(chips), key=lambda k: (k > 0, k % 2, k))
    contract = (((0,), (0,)), ((), ()))

    def dot(x, c):
        return jnp.dot(x, c, preferred_element_type=f32)

    def columns(k, side):
        start = ((chip ^ k) * 2 + (core ^ side)) * mine
        return lax.dynamic_slice_in_dim(expression, start, mine, 1)

    coef_copy, response_rows = together(coef_init.astype(bf16), responses.astype(f32))
    coef_other = core_swap(coef_copy, "coef_core")
    pairs = [jnp.stack([columns(k, 0), columns(k, 1)]) for k in range(chips)]
    for k in far_first:
        pairs[k] = chip_swap(pairs[k], k, f"cells{k}")
    weights = jnp.broadcast_to(penalty[:, None], coef_init.shape)

    def fit(k):
        return dot(pairs[k][0], coef_copy) + dot(pairs[k][1], coef_other)

    total = fit(0)
    leaving = {}
    before = ()
    for k in far_first:
        if before:
            pairs[k], *_ = together(pairs[k], *before)
        leaving[k] = fit(k).astype(bf16)
        before = (leaving[k],)
    own = jnp.concatenate([pairs[k][0] for k in order])
    other = jnp.concatenate([pairs[k][1] for k in order])

    coef = coef_init
    dual = dual_init
    for step in range(ITERS):
        merged = coef + dual
        squares = merged * merged
        if cond_bits > 0:
            squares = squares + cond_swap(squares.astype(bf16), 1, "squares0").astype(f32)
        if step == 0:
            held, squares, response_rows, *_ = together(other, squares, response_rows, *before)
        else:
            coef_copy = coef.astype(bf16)
            coef_other = core_swap(coef_copy, "coef_core")
            fitted = (dot(own, coef_copy) + dot(other, coef_other)).reshape(chips, cells, targets)
            total = fitted[0]
            leaving = {k: fitted[order.index(k)].astype(bf16) for k in far_first}
        arrived = [chip_swap(leaving[k], k, f"fit{k}") for k in far_first]
        for bit in range(1, cond_bits):
            squares = squares + cond_swap(squares.astype(bf16), 1 << bit, f"squares{bit}").astype(f32)
        total = total - response_rows
        for part in arrived:
            total = total + part.astype(f32)
        residual = [total.astype(bf16)] * chips
        for k in far_first:
            residual[k] = chip_swap(residual[0], k, f"residual{k}")
        if step == 0:
            across = core_swap(held, "cells_core")
            diagonal = jnp.sum(jnp.square(own.astype(f32)), 0) + jnp.sum(jnp.square(across.astype(f32)), 0)
            step_size = 1.0 / (diagonal / n_cells + rho_weight)[:, None]
        squares, step_size, across, weights, *ready = together(squares, step_size, across, weights, *[residual[k] for k in evens_first])
        residual = dict(zip(evens_first, ready))
        residual = jnp.concatenate([residual[k] for k in order])
        residual_other = core_swap(residual, "residual_core")
        norms = jnp.sqrt(squares)
        consensus = merged * (1.0 - weights / jnp.maximum(norms, weights))
        dual = merged - consensus
        scale = step_size / n_cells
        coef = coef + (rho_weight * (consensus - dual) - rho_weight * coef) * step_size
        coef = coef - lax.dot_general(own, residual, contract, preferred_element_type=f32) * scale
        if step < ITERS - 1:
            residual_other, coef, dual = together(residual_other, coef, dual)
        coef = coef - lax.dot_general(across, residual_other, contract, preferred_element_type=f32) * scale
    return (coef, consensus, dual)


def solution(mesh):
    in_specs = (
        P(("cond", "shard"), None),
        P(("cond", "shard"), None),
        P(("cond", "shard"), None),
        P(("cond", "shard"), None),
        P("shard"),
    )
    out_specs = (P(("cond", "shard"), None), P(("cond", "shard"), None), P(("cond", "shard"), None))
    return jax.shard_map(shards, mesh=mesh, in_specs=in_specs, out_specs=out_specs, check_vma=False)
```
